256 devices in a mesh: dp: 32 (over x_lo, z, core), expert: 8 (over x_hi, y).
Axes of the slice: x: 4 (x_hi: 2, x_lo: 2; x = x_hi * 2 + x_lo), y: 4, z: 8, core: 2. Of those that a mesh axis runs over, the one named last changes fastest.
Arguments:
- tokens: bfloat16 [32768, 3584], P(('dp', 'expert')), may hold values from -6 to 6
- cotangent: bfloat16 [32768, 3584], P(('dp', 'expert')), may hold values from -6 to 6
- experts: int32 [32768, 2], P(('dp', 'expert')), may hold values from 0 to 63, all different within a row
- route_weight: float32 [32768, 2], P(('dp', 'expert')), may hold values from 0.05 to 1
- w_gate: bfloat16 [8, 7168, 3584], P('expert', 'dp'), may hold values from -0.09375 to 0.09375
- w_up: bfloat16 [8, 7168, 3584], P('expert', 'dp'), may hold values from -0.09375 to 0.09375
- w_down: bfloat16 [8, 7168, 3584], P('expert', 'dp'), may hold values from -0.0625 to 0.0625
Outputs:
- token_grad: bfloat16 [32768, 3584], P(('dp', 'expert'))
- grad_gate: bfloat16 [8, 7168, 3584], P('expert', 'dp')
- grad_up: bfloat16 [8, 7168, 3584], P('expert', 'dp')
- grad_down: bfloat16 [8, 7168, 3584], P('expert', 'dp')
The draws below stay inside these ranges and needn't reach their ends.
Inputs may be any that keep to these rules, and one draw needn't show every extreme that they name: Each token names 2 different experts of the 64.
All inputs are finite; a program needn't handle non-finite values.
Results may differ from the reference program's by a relative error of at most 0.024.
Values may be sent and summed in bfloat16 or wider, within the bound.
No kernel may reach another device: no remote copies, remote signals or barrier semaphores. Data moves between devices by JAX's collectives and lax.ppermute only.
A program may use at most 128 MiB of HBM per device.

```python
import jax
import jax.numpy as jnp
from jax import lax

D = 3584
FF = 7168
ALL_EXPERTS = 64
TOP = 2
TOK_DEV = 128
CAP = 4
WINDOW = 8
TOKENS = 32768
N_DP = 32


def levels(own_key, shape, split, low, top_value):
    def one(dim, blocks):
        steps = jax.random.uniform(jax.random.fold_in(jax.random.fold_in(own_key, 6), dim), (blocks,), jnp.float32, low / len(split), top_value / len(split))
        return jnp.repeat(jnp.exp(steps), shape[dim] // blocks).reshape((-1,) + (1,) * (len(shape) - dim - 1))

    level = one(*split[0])
    for cut in split[1:]:
        level = level * one(*cut)
    return level


def picks_of(stream_key, rows, amount, top, lift):
    sequence = jax.random.permutation(jax.random.fold_in(stream_key, 1), amount)
    boost = sequence
    for power in range(3):
        boost = boost * boost // amount
    boost = boost * lift // amount
    chance = jax.random.randint(jax.random.fold_in(stream_key, 2), (rows, amount), 0, 4096) + boost
    fixed_rows = jax.random.permutation(jax.random.fold_in(stream_key, 3), rows)[jnp.arange(amount) % rows]
    chance = jnp.where(jnp.arange(rows)[:, None] == fixed_rows[None, :], 1 << 14, chance)
    priority = chance * amount + jnp.arange(amount)
    return lax.top_k(priority.astype(jnp.int32), top)[1].astype(jnp.int32)


def gaussian(rng, extent, spread, limit, shards=(), kind=jnp.bfloat16):
    entries = jax.random.normal(rng, extent, jnp.float32) * spread
    if len(shards) > 0:
        entries = levels(rng, extent, shards, -0.22, 0.18) * entries
    return jnp.clip(entries, min=-limit, max=limit).astype(kind)


def setup_inputs(seed: int = 0) -> dict:
    arg_keys = jax.random.split(jax.random.key(seed), 8)
    tokens = gaussian(arg_keys[0], (TOKENS, D), 1.0, 6.0, ((0, 256),))
    cotangent = gaussian(arg_keys[1], (TOKENS, D), 1.0, 6.0, ((0, 256),))
    experts = picks_of(arg_keys[2], TOKENS, ALL_EXPERTS, TOP, 256)
    route_weight = jnp.clip(0.05 + 0.95 * jax.random.uniform(arg_keys[3], (TOKENS, TOP), jnp.float32) ** levels(arg_keys[3], (TOKENS, TOP), ((0, 256),), -0.2, 0.2), 0.05, 1.0)
    w_gate = gaussian(arg_keys[4], (WINDOW, FF, D), D ** -0.5, 0.09375, ((0, 8), (1, 32)))
    w_up = gaussian(arg_keys[5], (WINDOW, FF, D), D ** -0.5, 0.09375, ((0, 8), (1, 32)))
    w_down = gaussian(arg_keys[6], (WINDOW, FF, D), FF ** -0.5, 0.0625, ((0, 8), (1, 32)))
    return dict(tokens=tokens, cotangent=cotangent, experts=experts, route_weight=route_weight, w_gate=w_gate, w_up=w_up, w_down=w_down)


def slot_table(experts_local, window, capacity):
    flat = experts_local.reshape(-1).astype(jnp.int32)
    count = flat.shape[0]
    labels = jnp.arange(window, dtype=jnp.int32)
    onehot = (flat[:, None] == labels[None, :]).astype(jnp.int32)
    before = jnp.cumsum(onehot, axis=0) - onehot
    slot = jnp.sum(before * onehot, axis=1).astype(jnp.int32)
    keep = (jnp.sum(onehot, axis=1) > 0) & (slot < capacity)
    target = jnp.where(keep, flat * capacity + slot, -1)
    places = jnp.arange(window * capacity, dtype=jnp.int32)
    match = (target[None, :] == places[:, None]).astype(jnp.int32)
    source = jnp.sum(match * jnp.arange(count, dtype=jnp.int32)[None, :], axis=1).astype(jnp.int32)
    filled = jnp.sum(match, axis=1) > 0
    return flat, slot, keep, source, filled


def fill_slots(tokens_local, cot_local, weight_flat, source, filled, top):
    which = source // top
    x_slots = jnp.where(filled[:, None], tokens_local[which], jnp.zeros((), tokens_local.dtype))
    scaled = weight_flat[source][:, None] * cot_local[which].astype(jnp.float32)
    c_slots = jnp.where(filled[:, None], scaled, jnp.float32(0.0)).astype(jnp.bfloat16)
    return x_slots, c_slots


def gather_back(slot_grad_local, flat, slot, keep, capacity, top):
    index = jnp.where(keep, flat * capacity + slot, 0).astype(jnp.int32)
    picked = jnp.where(keep[:, None], slot_grad_local[index].astype(jnp.float32), jnp.float32(0.0))
    return picked.reshape(-1, top, picked.shape[-1]).sum(axis=1).astype(jnp.bfloat16)


def reference(tokens, cotangent, experts, route_weight, w_gate, w_up, w_down):
    blocks = TOKENS // TOK_DEV
    tok_blocks = tokens.reshape(blocks, TOK_DEV, D)
    cot_blocks = cotangent.reshape(blocks, TOK_DEV, D)
    exp_blocks = experts.reshape(blocks, TOK_DEV, TOP)
    wt_blocks = route_weight.reshape(blocks, TOK_DEV * TOP)
    flat, slot, keep, source, filled = jax.vmap(lambda e: slot_table(e, WINDOW, CAP))(exp_blocks)
    x_slots, c_slots = jax.vmap(lambda t, c, w, s, f: fill_slots(t, c, w, s, f, TOP))(tok_blocks, cot_blocks, wt_blocks, source, filled)
    x_all = x_slots.reshape(blocks, WINDOW, CAP, D)
    c_all = c_slots.reshape(blocks, WINDOW, CAP, D)
    group = FF // N_DP
    grads_gate = []
    grads_up = []
    grads_down = []
    slot_parts = []
    for expert in range(WINDOW):
        x_rows = x_all[:, expert].reshape(-1, D)
        c_rows = c_all[:, expert].reshape(-1, D)
        gate = jnp.dot(x_rows, w_gate[expert].T, preferred_element_type=jnp.float32)
        up = jnp.dot(x_rows, w_up[expert].T, preferred_element_type=jnp.float32)
        sig = jax.nn.sigmoid(gate)
        act = gate * sig
        hidden = (act * up).astype(jnp.bfloat16)
        back = jnp.dot(c_rows, w_down[expert].T, preferred_element_type=jnp.float32)
        d_gate = (back * up * sig * (1.0 + gate * (1.0 - sig))).astype(jnp.bfloat16)
        d_up = (back * act).astype(jnp.bfloat16)
        grads_gate.append(jnp.dot(d_gate.T, x_rows, preferred_element_type=jnp.float32).astype(jnp.bfloat16))
        grads_up.append(jnp.dot(d_up.T, x_rows, preferred_element_type=jnp.float32).astype(jnp.bfloat16))
        grads_down.append(jnp.dot(hidden.T, c_rows, preferred_element_type=jnp.float32).astype(jnp.bfloat16))
        total = jnp.zeros((x_rows.shape[0], D), jnp.float32)
        for index in range(N_DP):
            lo = index * group
            hi = lo + group
            part = jnp.dot(d_gate[:, lo:hi], w_gate[expert][lo:hi], preferred_element_type=jnp.float32) + jnp.dot(d_up[:, lo:hi], w_up[expert][lo:hi], preferred_element_type=jnp.float32)
            total = total + part.astype(jnp.bfloat16).astype(jnp.float32)
        slot_parts.append(total.astype(jnp.bfloat16).reshape(blocks, CAP, D))
    slot_grad = jnp.stack(slot_parts, axis=1).reshape(blocks, WINDOW * CAP, D)
    token_grad = jax.vmap(lambda g, f, s, k: gather_back(g, f, s, k, CAP, TOP))(slot_grad, flat, slot, keep)
    return (token_grad.reshape(TOKENS, D), jnp.stack(grads_gate), jnp.stack(grads_up), jnp.stack(grads_down))
```

```python
import jax
import jax.numpy as jnp
from jax import lax
from jax.sharding import Mesh
from jax.sharding import PartitionSpec as P

CAP = 4
DP = ("xlo", "z", "core")
DP_EXPERT = ("xlo", "z", "core", "expert")
SWAP = ((0, 1), (1, 0))


def matmul(a, b, dims):
    return lax.dot_general(a, b, (dims, ((), ())), preferred_element_type=jnp.float32)


def shift(x, by):
    size = lax.axis_size("z")
    return lax.ppermute(x, "z", [(i, (i + by) % size) for i in range(size)])


def across(x):
    return lax.ppermute(x, "xlo", SWAP)


def partner(x):
    return lax.ppermute(x, "core", SWAP)


def routing(experts, route_weight, window):
    chosen = experts.T
    weight = route_weight.T
    count = chosen.shape[1]
    hit = chosen[None] == jnp.arange(window, dtype=jnp.int32)[:, None, None]
    named = hit[:, 0] | hit[:, 1]
    row = lax.broadcasted_iota(jnp.int32, (count, count), 0)
    col = lax.broadcasted_iota(jnp.int32, (count, count), 1)
    before = matmul(named.astype(jnp.bfloat16), (row < col).astype(jnp.bfloat16), ((1,), (0,)))
    slots = jnp.arange(CAP, dtype=jnp.float32)
    picked = named[:, None, :] & (before[:, None, :] == slots[None, :, None])
    own = jnp.where(hit[:, 0], weight[0], jnp.where(hit[:, 1], weight[1], 0.0))
    scale = jnp.sum(jnp.where(picked, own[:, None, :], 0.0), axis=2)
    return picked.astype(jnp.bfloat16), scale


def terms(x, c, gate_w, up_w, down_w):
    gate = matmul(x, gate_w, ((1,), (1,)))
    up = matmul(x, up_w, ((1,), (1,)))
    sig = jax.nn.sigmoid(gate)
    act = gate * sig
    hidden = (act * up).astype(jnp.bfloat16)
    back = matmul(c, down_w, ((1,), (1,)))
    d_gate = (back * up * sig * (1.0 + gate * (1.0 - sig))).astype(jnp.bfloat16)
    d_up = (back * act).astype(jnp.bfloat16)
    part = matmul(d_gate, gate_w, ((1,), (0,))) + matmul(d_up, up_w, ((1,), (0,)))
    return hidden, d_gate, d_up, part.astype(jnp.bfloat16)


def added(a, b):
    return (a.astype(jnp.float32) + b.astype(jnp.float32)).astype(jnp.bfloat16)


def shards(tokens, cotangent, experts, route_weight, w_gate, w_up, w_down):
    window = lax.axis_size("expert")
    width = tokens.shape[1]
    units = w_gate.shape[1]
    both_w = [jnp.concatenate([w[0], partner(w[0])], axis=0) for w in (w_gate, w_up, w_down)]

    picked, scale = routing(experts, route_weight, window)
    select = picked.reshape(window * CAP, -1)
    x_send = matmul(select, tokens, ((1,), (0,))).astype(jnp.bfloat16)
    c_send = scale.reshape(-1, 1) * matmul(select, cotangent, ((1,), (0,)))
    c_send = c_send.astype(jnp.bfloat16)
    send = jnp.concatenate(
        [x_send.reshape(window, CAP, width), c_send.reshape(window, CAP, width)], axis=1
    )
    got = lax.all_to_all(send, "expert", split_axis=0, concat_axis=0, tiled=True)
    x_own = got[:, :CAP].reshape(-1, width)
    c_own = got[:, CAP:].reshape(-1, width)
    rows = x_own.shape[0]

    start = jnp.concatenate([c_own, across(c_own), x_own], axis=0)
    half = start.shape[0] // 2
    blocks = {0: start}
    for step in (1, 2, 3):
        blocks[-step] = shift(blocks[1 - step], 1)
        blocks[step] = shift(blocks[step - 1], -1)
    blocks[4] = jnp.concatenate(
        [shift(blocks[-3][:half], 1), shift(blocks[3][half:], -1)], axis=0
    )

    def rows_of(at):
        b = blocks[at]
        x_mine = b[2 * rows :]
        return b[: 2 * rows], jnp.concatenate([x_mine, across(x_mine)], axis=0)

    parts, hs, gs, us, xs, cs = {}, [], [], [], [], []
    for group in ((0, 1, -1, 2, -2), (3, -3, 4)):
        pairs = [rows_of(at) for at in group]
        c = jnp.concatenate([p[0] for p in pairs], axis=0)
        x = jnp.concatenate([p[1] for p in pairs], axis=0)
        hidden, d_gate, d_up, part = terms(x, c, *both_w)
        for i, at in enumerate(group):
            parts[at] = part[i * 2 * rows : (i + 1) * 2 * rows]
        hs.append(hidden)
        gs.append(d_gate)
        us.append(d_up)
        xs.append(x)
        cs.append(c)

    up = shift(parts[4][:rows], 1)
    up = jnp.concatenate([added(parts[3][:rows], up), parts[3][rows:]], axis=0)
    down = shift(parts[4][rows:], -1)
    down = jnp.concatenate([parts[-3][:rows], added(parts[-3][rows:], down)], axis=0)
    for step in (2, 1):
        up = added(parts[step], shift(up, 1))
        down = added(parts[-step], shift(down, -1))
    total = (
        parts[0].astype(jnp.float32)
        + shift(up, 1).astype(jnp.float32)
        + shift(down, -1).astype(jnp.float32)
    )
    other = across(total[rows:].astype(jnp.bfloat16))
    slot_grad = (total[:rows] + other.astype(jnp.float32)).astype(jnp.bfloat16)
    returned = lax.all_to_all(
        slot_grad.reshape(window, CAP, width), "expert", split_axis=0, concat_axis=0, tiled=True
    ).reshape(window * CAP, width)
    token_grad = matmul(select, returned, ((0,), (0,))).astype(jnp.bfloat16)

    grads = []
    for left, right in ((gs, xs), (us, xs), (hs, cs)):
        mine, theirs = 0.0, 0.0
        for a, b in zip(left, right):
            mine = mine + matmul(a[:, :units], b, ((0,), (0,)))
            theirs = theirs + matmul(a[:, units:], b, ((0,), (0,)))
        came = partner(theirs.astype(jnp.bfloat16))
        grads.append((mine + came.astype(jnp.float32)).astype(jnp.bfloat16)[None])
    return (token_grad, *grads)


def solution(mesh):
    split = Mesh(mesh.devices.reshape(2, 8, 2, mesh.shape["expert"]), DP_EXPERT)
    tok = P(DP_EXPERT, None)
    wts = P("expert", DP, None)
    return jax.shard_map(
        shards,
        mesh=split,
        in_specs=(tok, tok, tok, tok, wts, wts, wts),
        out_specs=(tok, wts, wts, wts),
        check_vma=False,
    )
```

```python
import jax
import jax.numpy as jnp
from jax import lax
from jax.sharding import Mesh
from jax.sharding import PartitionSpec as P

CAP = 4
DP = ("xlo", "z", "core")
DP_EXPERT = ("xlo", "z", "core", "expert")
SWAP = ((0, 1), (1, 0))


def matmul(a, b, dims):
    return lax.dot_general(a, b, (dims, ((), ())), preferred_element_type=jnp.float32)


def shift(x, by):
    size = lax.axis_size("z")
    return lax.ppermute(x, "z", [(i, (i + by) % size) for i in range(size)])


def across(x):
    return lax.ppermute(x, "xlo", SWAP)


def partner(x):
    return lax.ppermute(x, "core", SWAP)


def routing(experts, route_weight, window):
    chosen = experts.T
    weight = route_weight.T
    count = chosen.shape[1]
    hit = chosen[None] == jnp.arange(window, dtype=jnp.int32)[:, None, None]
    named = hit[:, 0] | hit[:, 1]
    row = lax.broadcasted_iota(jnp.int32, (count, count), 0)
    col = lax.broadcasted_iota(jnp.int32, (count, count), 1)
    before = matmul(named.astype(jnp.bfloat16), (row < col).astype(jnp.bfloat16), ((1,), (0,)))
    slots = jnp.arange(CAP, dtype=jnp.float32)
    picked = named[:, None, :] & (before[:, None, :] == slots[None, :, None])
    own = jnp.where(hit[:, 0], weight[0], jnp.where(hit[:, 1], weight[1], 0.0))
    scale = jnp.sum(jnp.where(picked, own[:, None, :], 0.0), axis=2)
    return picked.astype(jnp.bfloat16), scale


def terms(x, c, gate_w, up_w, down_w):
    gate = matmul(x, gate_w, ((1,), (1,)))
    up = matmul(x, up_w, ((1,), (1,)))
    sig = jax.nn.sigmoid(gate)
    act = gate * sig
    hidden = (act * up).astype(jnp.bfloat16)
    back = matmul(c, down_w, ((1,), (1,)))
    d_gate = (back * up * sig * (1.0 + gate * (1.0 - sig))).astype(jnp.bfloat16)
    d_up = (back * act).astype(jnp.bfloat16)
    part = matmul(d_gate, gate_w, ((1,), (0,))) + matmul(d_up, up_w, ((1,), (0,)))
    return hidden, d_gate, d_up, part.astype(jnp.bfloat16)


def added(a, b):
    return (a.astype(jnp.float32) + b.astype(jnp.float32)).astype(jnp.bfloat16)


def shards(tokens, cotangent, experts, route_weight, w_gate, w_up, w_down):
    window = lax.axis_size("expert")
    width = tokens.shape[1]
    units = w_gate.shape[1]
    both_w = [jnp.concatenate([w[0], partner(w[0])], axis=0) for w in (w_gate, w_up, w_down)]

    picked, scale = routing(experts, route_weight, window)
    select = picked.reshape(window * CAP, -1)
    x_send = matmul(select, tokens, ((1,), (0,))).astype(jnp.bfloat16)
    c_send = scale.reshape(-1, 1) * matmul(select, cotangent, ((1,), (0,)))
    c_send = c_send.astype(jnp.bfloat16)
    send = jnp.concatenate(
        [x_send.reshape(window, CAP, width), c_send.reshape(window, CAP, width)], axis=1
    )
    got = lax.all_to_all(send, "expert", split_axis=0, concat_axis=0, tiled=True)
    x_own = got[:, :CAP].reshape(-1, width)
    c_own = got[:, CAP:].reshape(-1, width)
    rows = x_own.shape[0]

    near = jnp.concatenate([c_own, x_own], axis=0)
    far = across(c_own)
    cut = rows // 2
    first, second, crossed = {0: near}, {0: far}, {0: across(x_own)}
    for step in (1, 2, 3):
        for at, by in ((-step, 1), (step, -1)):
            first[at] = shift(first[at + by], by)
            second[at] = shift(second[at + by], by)
            crossed[at] = across(first[at][rows:])
    first[4] = jnp.concatenate([shift(first[-3][:rows], 1), shift(first[3][rows:], -1)], axis=0)
    second[4] = jnp.concatenate([shift(second[-3][:cut], 1), shift(second[3][cut:], -1)], axis=0)
    crossed[4] = across(first[4][rows:])

    parts, hs, gs, us, xs, cs = {}, [], [], [], [], []
    for group in ((0, 1, -1, 2, -2), (3, -3, 4)):
        c = jnp.concatenate([p for at in group for p in (first[at][:rows], second[at])], axis=0)
        x = jnp.concatenate([p for at in group for p in (first[at][rows:], crossed[at])], axis=0)
        hidden, d_gate, d_up, part = terms(x, c, *both_w)
        for i, at in enumerate(group):
            parts[at] = part[i * 2 * rows : (i + 1) * 2 * rows]
        hs.append(hidden)
        gs.append(d_gate)
        us.append(d_up)
        xs.append(x)
        cs.append(c)

    pieces = []
    for lo, hi in ((0, width // 2), (width // 2, width)):
        p = {at: v[:, lo:hi] for at, v in parts.items()}
        up = shift(p[4][:rows], 1)
        up = jnp.concatenate([added(p[3][:rows], up), p[3][rows:]], axis=0)
        down = shift(p[4][rows:], -1)
        down = jnp.concatenate([p[-3][:rows], added(p[-3][rows:], down)], axis=0)
        for step in (2, 1):
            up = added(p[step], shift(up, 1))
            down = added(p[-step], shift(down, -1))
        total = (
            p[0].astype(jnp.float32)
            + shift(up, 1).astype(jnp.float32)
            + shift(down, -1).astype(jnp.float32)
        )
        other = across(total[rows:].astype(jnp.bfloat16))
        pieces.append((total[:rows] + other.astype(jnp.float32)).astype(jnp.bfloat16))
    slot_grad = jnp.concatenate(pieces, axis=1)
    returned = lax.all_to_all(
        slot_grad.reshape(window, CAP, width), "expert", split_axis=0, concat_axis=0, tiled=True
    ).reshape(window * CAP, width)
    token_grad = matmul(select, returned, ((0,), (0,))).astype(jnp.bfloat16)

    grads = []
    for left, right in ((gs, xs), (us, xs), (hs, cs)):
        whole = 0.0
        for a, b in zip(left, right):
            whole = whole + matmul(a, b, ((0,), (0,)))
        whole = whole.astype(jnp.bfloat16)
        grads.append(added(whole[:units], partner(whole[units:]))[None])
    return (token_grad, *grads)


def solution(mesh):
    split = Mesh(mesh.devices.reshape(2, 8, 2, mesh.shape["expert"]), DP_EXPERT)
    tok = P(DP_EXPERT, None)
    wts = P("expert", DP, None)
    return jax.shard_map(
        shards,
        mesh=split,
        in_specs=(tok, tok, tok, tok, wts, wts, wts),
        out_specs=(tok, wts, wts, wts),
        check_vma=False,
    )
```

```python
import jax
import jax.numpy as jnp
from jax import lax
from jax.sharding import Mesh
from jax.sharding import PartitionSpec as P


CAP = 4
DP = ("xlo", "z", "core")
DP_EXPERT = ("xlo", "z", "core", "expert")
SWAP = ((0, 1), (1, 0))


def matmul(a, b, dims):
    return lax.dot_general(a, b, (dims, ((), ())), preferred_element_type=jnp.float32)


def shift(x, by):
    size = lax.axis_size("z")
    return lax.ppermute(x, "z", [(i, (i + by) % size) for i in range(size)])


def across(x):
    return lax.ppermute(x, "xlo", SWAP)


def partner(x):
    return lax.ppermute(x, "core", SWAP)


def routing(experts, route_weight, window):
    chosen = experts.T
    weight = route_weight.T
    count = chosen.shape[1]
    hit = chosen[None] == jnp.arange(window, dtype=jnp.int32)[:, None, None]
    named = hit[:, 0] | hit[:, 1]
    row = lax.broadcasted_iota(jnp.int32, (count, count), 0)
    col = lax.broadcasted_iota(jnp.int32, (count, count), 1)
    before = matmul(named.astype(jnp.bfloat16), (row < col).astype(jnp.bfloat16), ((1,), (0,)))
    slots = jnp.arange(CAP, dtype=jnp.float32)
    picked = named[:, None, :] & (before[:, None, :] == slots[None, :, None])
    own = jnp.where(hit[:, 0], weight[0], jnp.where(hit[:, 1], weight[1], 0.0))
    scale = jnp.sum(jnp.where(picked, own[:, None, :], 0.0), axis=2)
    return picked.astype(jnp.bfloat16), scale


def terms(x, c, gate_w, up_w, down_w):
    gate = matmul(x, gate_w, ((1,), (1,)))
    up = matmul(x, up_w, ((1,), (1,)))
    sig = jax.nn.sigmoid(gate)
    act = gate * sig
    hidden = (act * up).astype(jnp.bfloat16)
    back = matmul(c, down_w, ((1,), (1,)))
    d_gate = (back * up * sig * (1.0 + gate * (1.0 - sig))).astype(jnp.bfloat16)
    d_up = (back * act).astype(jnp.bfloat16)
    part = matmul(d_gate, gate_w, ((1,), (0,))) + matmul(d_up, up_w, ((1,), (0,)))
    return hidden, d_gate, d_up, part.astype(jnp.bfloat16)


def added(a, b):
    return (a.astype(jnp.float32) + b.astype(jnp.float32)).astype(jnp.bfloat16)


def shards(tokens, cotangent, experts, route_weight, w_gate, w_up, w_down):
    window = lax.axis_size("expert")
    width = tokens.shape[1]
    units = w_gate.shape[1]
    came_w = [partner(w[0]) for w in (w_gate, w_up, w_down)]
    both_w = [
        jnp.concatenate([w[0], came], axis=0)
        for w, came in zip((w_gate, w_up, w_down), came_w)
    ]
    both_w = lax.optimization_barrier(both_w)
    picked, scale = routing(experts, route_weight, window)
    select = picked.reshape(window * CAP, -1)
    x_send = matmul(select, tokens, ((1,), (0,))).astype(jnp.bfloat16)
    c_send = scale.reshape(-1, 1) * matmul(select, cotangent, ((1,), (0,)))
    c_send = c_send.astype(jnp.bfloat16)
    send = jnp.concatenate(
        [x_send.reshape(window, CAP, width), c_send.reshape(window, CAP, width)], axis=1
    )
    got = lax.all_to_all(send, "expert", split_axis=0, concat_axis=0, tiled=True)
    x_own = got[:, :CAP].reshape(-1, width)
    c_own = got[:, CAP:].reshape(-1, width)
    rows = x_own.shape[0]

    half = rows // 2
    first, second, crossed = {0: jnp.concatenate([c_own, x_own], axis=0)}, {}, {}

    def cross(*at):
        sent = across(jnp.concatenate([first[i][rows:] for i in at], axis=0))
        for n, i in enumerate(at):
            crossed[i] = sent[n * rows : (n + 1) * rows]

    second[0] = across(c_own)
    cross(0)
    for step in (1, 2, 3):
        for at, by in ((-step, 1), (step, -1)):
            first[at] = shift(first[at + by], by)
            second[at] = shift(second[at + by], by)
        cross(-step, step)
    first[4] = jnp.concatenate([shift(first[-3][:rows], 1), shift(first[3][rows:], -1)], axis=0)
    second[4] = jnp.concatenate([shift(second[-3][:half], 1), shift(second[3][half:], -1)], axis=0)
    cross(4)

    cut = width // 2 - 128
    sides = (("left", 0, cut), ("right", cut, width))
    parts, hs, gs, us, xs, cs = {}, [], [], [], [], []
    for group in ((0, 1, -1, 2, -2), (3, -3, 4)):
        kept = {at: lax.optimization_barrier(first[at]) for at in group}
        c = jnp.concatenate(
            [p for at in group for p in (kept[at][:rows], second[at])], axis=0
        )
        x = jnp.concatenate(
            [p for at in group for p in (kept[at][rows:], crossed[at])], axis=0
        )
        hidden, d_gate, d_up, part = terms(x, c, *both_w)
        pieces = {
            (at, side): part[i * 2 * rows : (i + 1) * 2 * rows, lo:hi]
            for i, at in enumerate(group)
            for side, lo, hi in sides
        }
        parts.update(lax.optimization_barrier(pieces))
        hs.append(hidden)
        gs.append(d_gate)
        us.append(d_up)
        xs.append(x)
        cs.append(c)

    totals = []
    for side, _, _ in sides:
        p = {at: parts[at, side] for at in range(-3, 5)}
        up = shift(p[4][:rows], 1)
        up = jnp.concatenate([added(p[3][:rows], up), p[3][rows:]], axis=0)
        down = shift(p[4][rows:], -1)
        down = jnp.concatenate([p[-3][:rows], added(p[-3][rows:], down)], axis=0)
        for step in (2, 1):
            up = added(p[step], shift(up, 1))
            down = added(p[-step], shift(down, -1))
        totals.append(
            p[0].astype(jnp.float32)
            + shift(up, 1).astype(jnp.float32)
            + shift(down, -1).astype(jnp.float32)
        )
    total = jnp.concatenate(totals, axis=1)
    other = across(total[rows:].astype(jnp.bfloat16))
    slot_grad = (total[:rows] + other.astype(jnp.float32)).astype(jnp.bfloat16)
    returned = lax.all_to_all(
        slot_grad.reshape(window, CAP, width), "expert", split_axis=0, concat_axis=0, tiled=True
    ).reshape(window * CAP, width)
    token_grad = matmul(select, returned, ((0,), (0,))).astype(jnp.bfloat16)

    grads = []
    for left, right in ((gs, xs), (us, xs), (hs, cs)):
        whole = 0.0
        for a, b in zip(left, right):
            whole = whole + matmul(a, b, ((0,), (0,)))
        whole = whole.astype(jnp.bfloat16)
        grads.append(added(whole[:units], partner(whole[units:]))[None])
    return (token_grad, *grads)


def solution(mesh):
    split = Mesh(mesh.devices.reshape(2, 8, 2, mesh.shape["expert"]), DP_EXPERT)
    tok = P(DP_EXPERT, None)
    wts = P("expert", DP, None)
    return jax.shard_map(
        shards,
        mesh=split,
        in_specs=(tok, tok, tok, tok, wts, wts, wts),
        out_specs=(tok, wts, wts, wts),
        check_vma=False,
    )
```

```python
import jax
import jax.numpy as jnp
from jax import lax
from jax.sharding import Mesh
from jax.sharding import PartitionSpec as P


CAP = 4
DP = ("xlo", "z", "core")
DP_EXPERT = ("xlo", "z", "core", "expert")
SWAP = ((0, 1), (1, 0))


def matmul(a, b, dims):
    return lax.dot_general(a, b, (dims, ((), ())), preferred_element_type=jnp.float32)


def shift(x, by):
    size = lax.axis_size("z")
    return lax.ppermute(x, "z", [(i, (i + by) % size) for i in range(size)])


def across(x):
    return lax.ppermute(x, "xlo", SWAP)


def partner(x):
    return lax.ppermute(x, "core", SWAP)


def routing(experts, route_weight, window):
    chosen = experts.T
    weight = route_weight.T
    count = chosen.shape[1]
    hit = chosen[None] == jnp.arange(window, dtype=jnp.int32)[:, None, None]
    named = hit[:, 0] | hit[:, 1]
    row = lax.broadcasted_iota(jnp.int32, (count, count), 0)
    col = lax.broadcasted_iota(jnp.int32, (count, count), 1)
    before = matmul(named.astype(jnp.bfloat16), (row < col).astype(jnp.bfloat16), ((1,), (0,)))
    slots = jnp.arange(CAP, dtype=jnp.float32)
    picked = named[:, None, :] & (before[:, None, :] == slots[None, :, None])
    own = jnp.where(hit[:, 0], weight[0], jnp.where(hit[:, 1], weight[1], 0.0))
    scale = jnp.sum(jnp.where(picked, own[:, None, :], 0.0), axis=2)
    return picked.astype(jnp.bfloat16), scale


def terms(x, c, gate_w, up_w, down_w):
    gate = matmul(x, gate_w, ((1,), (1,)))
    up = matmul(x, up_w, ((1,), (1,)))
    sig = jax.nn.sigmoid(gate)
    act = gate * sig
    hidden = (act * up).astype(jnp.bfloat16)
    back = matmul(c, down_w, ((1,), (1,)))
    d_gate = (back * up * sig * (1.0 + gate * (1.0 - sig))).astype(jnp.bfloat16)
    d_up = (back * act).astype(jnp.bfloat16)
    part = matmul(d_gate, gate_w, ((1,), (0,))) + matmul(d_up, up_w, ((1,), (0,)))
    return hidden, d_gate, d_up, part.astype(jnp.bfloat16)


def added(a, b):
    return (a.astype(jnp.float32) + b.astype(jnp.float32)).astype(jnp.bfloat16)


def shards(tokens, cotangent, experts, route_weight, w_gate, w_up, w_down):
    window = lax.axis_size("expert")
    width = tokens.shape[1]
    units = w_gate.shape[1]
    came_w = [partner(w[0]) for w in (w_gate, w_up, w_down)]
    both_w = [
        jnp.concatenate([w[0], came], axis=0)
        for w, came in zip((w_gate, w_up, w_down), came_w)
    ]
    both_w = lax.optimization_barrier(both_w)
    picked, scale = routing(experts, route_weight, window)
    select = picked.reshape(window * CAP, -1)
    x_send = matmul(select, tokens, ((1,), (0,))).astype(jnp.bfloat16)
    c_send = scale.reshape(-1, 1) * matmul(select, cotangent, ((1,), (0,)))
    c_send = c_send.astype(jnp.bfloat16)
    send = jnp.concatenate(
        [x_send.reshape(window, CAP, width), c_send.reshape(window, CAP, width)], axis=1
    )
    got = lax.all_to_all(send, "expert", split_axis=0, concat_axis=0, tiled=True)
    x_own = got[:, :CAP].reshape(-1, width)
    c_own = got[:, CAP:].reshape(-1, width)
    rows = x_own.shape[0]

    half = rows // 2
    first, second, crossed = {0: jnp.concatenate([c_own, x_own], axis=0)}, {}, {}

    def cross(*at):
        sent = across(jnp.concatenate([first[i][rows:] for i in at], axis=0))
        for n, i in enumerate(at):
            crossed[i] = sent[n * rows : (n + 1) * rows]

    second[0] = across(c_own)
    cross(0)
    for step in (1, 2, 3):
        for at, by in ((-step, 1), (step, -1)):
            first[at] = shift(first[at + by], by)
            second[at] = shift(second[at + by], by)
        cross(-step, step)
    first[4] = jnp.concatenate([shift(first[-3][:rows], 1), shift(first[3][rows:], -1)], axis=0)
    second[4] = jnp.concatenate([shift(second[-3][:half], 1), shift(second[3][half:], -1)], axis=0)
    cross(4)

    cut = width // 2 - 128
    sides = (("left", 0, cut), ("right", cut, width))
    parts, hs, gs, us, xs, cs = {}, [], [], [], [], []
    for group in ((0, 1, -1, 2, -2), (3, -3, 4)):
        kept = {at: lax.optimization_barrier(first[at]) for at in group}
        c = jnp.concatenate(
            [p for at in group for p in (kept[at][:rows], second[at])], axis=0
        )
        x = jnp.concatenate(
            [p for at in group for p in (kept[at][rows:], crossed[at])], axis=0
        )
        hidden, d_gate, d_up, part = terms(x, c, *both_w)
        pieces = {
            (at, side): part[i * 2 * rows : (i + 1) * 2 * rows, lo:hi]
            for i, at in enumerate(group)
            for side, lo, hi in sides
        }
        parts.update(lax.optimization_barrier(pieces))
        hs.append(hidden)
        gs.append(d_gate)
        us.append(d_up)
        xs.append(x)
        cs.append(c)

    totals = []
    for side, _, _ in sides:
        p = {at: parts[at, side] for at in range(-3, 5)}
        up = shift(p[4][:rows], 1)
        up = jnp.concatenate([added(p[3][:rows], up), p[3][rows:]], axis=0)
        down = shift(p[4][rows:], -1)
        down = jnp.concatenate([p[-3][:rows], added(p[-3][rows:], down)], axis=0)
        for step in (2, 1):
            up = added(p[step], shift(up, 1))
            down = added(p[-step], shift(down, -1))
        totals.append(
            p[0].astype(jnp.float32)
            + shift(up, 1).astype(jnp.float32)
            + shift(down, -1).astype(jnp.float32)
        )
    total = jnp.concatenate(totals, axis=1)
    other = across(total[rows:].astype(jnp.bfloat16))
    slot_grad = (total[:rows] + other.astype(jnp.float32)).astype(jnp.bfloat16)
    returned = lax.all_to_all(
        slot_grad.reshape(window, CAP, width), "expert", split_axis=0, concat_axis=0, tiled=True
    ).reshape(window * CAP, width)
    token_grad = matmul(select, returned, ((0,), (0,))).astype(jnp.bfloat16)

    grads = []
    for left, right in ((gs, xs), (us, xs), (hs, cs)):
        mine, theirs = 0.0, 0.0
        for a, b in zip(left, right):
            theirs = theirs + matmul(a[:, units:], b, ((0,), (0,)))
        came = partner(theirs.astype(jnp.bfloat16))
        for a, b in zip(left, right):
            mine = mine + matmul(a[:, :units], b, ((0,), (0,)))
        grads.append((mine + came.astype(jnp.float32)).astype(jnp.bfloat16)[None])
    return (token_grad, *grads)


def solution(mesh):
    split = Mesh(mesh.devices.reshape(2, 8, 2, mesh.shape["expert"]), DP_EXPERT)
    tok = P(DP_EXPERT, None)
    wts = P("expert", DP, None)
    return jax.shard_map(
        shards,
        mesh=split,
        in_specs=(tok, tok, tok, tok, wts, wts, wts),
        out_specs=(tok, wts, wts, wts),
        check_vma=False,
    )
```

```python
import jax
import jax.numpy as jnp
from jax import lax
from jax.sharding import Mesh
from jax.sharding import PartitionSpec as P


CAP = 4
DP = ("xlo", "z", "core")
DP_EXPERT = ("xlo", "z", "core", "expert")
SWAP = ((0, 1), (1, 0))


def matmul(a, b, dims):
    return lax.dot_general(a, b, (dims, ((), ())), preferred_element_type=jnp.float32)


def shift(x, by):
    size = lax.axis_size("z")
    return lax.ppermute(x, "z", [(i, (i + by) % size) for i in range(size)])


def across(x):
    return lax.ppermute(x, "xlo", SWAP)


def partner(x):
    return lax.ppermute(x, "core", SWAP)


def routing(experts, route_weight, window):
    chosen = experts.T
    weight = route_weight.T
    count = chosen.shape[1]
    hit = chosen[None] == jnp.arange(window, dtype=jnp.int32)[:, None, None]
    named = hit[:, 0] | hit[:, 1]
    row = lax.broadcasted_iota(jnp.int32, (count, count), 0)
    col = lax.broadcasted_iota(jnp.int32, (count, count), 1)
    before = matmul(named.astype(jnp.bfloat16), (row < col).astype(jnp.bfloat16), ((1,), (0,)))
    slots = jnp.arange(CAP, dtype=jnp.float32)
    picked = named[:, None, :] & (before[:, None, :] == slots[None, :, None])
    own = jnp.where(hit[:, 0], weight[0], jnp.where(hit[:, 1], weight[1], 0.0))
    scale = jnp.sum(jnp.where(picked, own[:, None, :], 0.0), axis=2)
    return picked.astype(jnp.bfloat16), scale


def terms(x, c, gate_w, up_w, down_w):
    gate = matmul(x, gate_w, ((1,), (1,)))
    up = matmul(x, up_w, ((1,), (1,)))
    sig = jax.nn.sigmoid(gate)
    act = gate * sig
    hidden = (act * up).astype(jnp.bfloat16)
    back = matmul(c, down_w, ((1,), (1,)))
    d_gate = (back * up * sig * (1.0 + gate * (1.0 - sig))).astype(jnp.bfloat16)
    d_up = (back * act).astype(jnp.bfloat16)
    part = matmul(d_gate, gate_w, ((1,), (0,))) + matmul(d_up, up_w, ((1,), (0,)))
    return hidden, d_gate, d_up, part.astype(jnp.bfloat16)


def added(a, b):
    return (a.astype(jnp.float32) + b.astype(jnp.float32)).astype(jnp.bfloat16)


def shards(tokens, cotangent, experts, route_weight, w_gate, w_up, w_down):
    window = lax.axis_size("expert")
    width = tokens.shape[1]
    units = w_gate.shape[1]
    came_w = [partner(w[0]) for w in (w_gate, w_up, w_down)]
    both_w = [
        jnp.concatenate([w[0], came], axis=0)
        for w, came in zip((w_gate, w_up, w_down), came_w)
    ]
    both_w = lax.optimization_barrier(both_w)
    picked, scale = routing(experts, route_weight, window)
    select = picked.reshape(window * CAP, -1)
    x_send = matmul(select, tokens, ((1,), (0,))).astype(jnp.bfloat16)
    c_send = scale.reshape(-1, 1) * matmul(select, cotangent, ((1,), (0,)))
    c_send = c_send.astype(jnp.bfloat16)
    send = jnp.concatenate(
        [x_send.reshape(window, CAP, width), c_send.reshape(window, CAP, width)], axis=1
    )
    got = lax.all_to_all(send, "expert", split_axis=0, concat_axis=0, tiled=True)
    x_own = got[:, :CAP].reshape(-1, width)
    c_own = got[:, CAP:].reshape(-1, width)
    rows = x_own.shape[0]

    half = rows // 2
    first, second, crossed = {0: jnp.concatenate([c_own, x_own], axis=0)}, {}, {}

    def cross(*at):
        sent = across(jnp.concatenate([first[i][rows:] for i in at], axis=0))
        for n, i in enumerate(at):
            crossed[i] = sent[n * rows : (n + 1) * rows]

    second[0] = across(c_own)
    cross(0)
    for step in (1, 2, 3):
        for at, by in ((-step, 1), (step, -1)):
            first[at] = shift(first[at + by], by)
            second[at] = shift(second[at + by], by)
        cross(-step, step)
    first[4] = jnp.concatenate([shift(first[-3][:rows], 1), shift(first[3][rows:], -1)], axis=0)
    second[4] = jnp.concatenate([shift(second[-3][:half], 1), shift(second[3][half:], -1)], axis=0)
    cross(4)

    cut = width // 2 - 128
    sides = (("left", 0, cut), ("right", cut, width))
    parts, hs, gs, us, xs, cs = {}, [], [], [], [], []
    for group in ((0, 1, -1, 2, -2), (3, -3, 4)):
        kept = {at: lax.optimization_barrier(first[at]) for at in group}
        c = jnp.concatenate(
            [p for at in group for p in (kept[at][:rows], second[at])], axis=0
        )
        x = jnp.concatenate(
            [p for at in group for p in (kept[at][rows:], crossed[at])], axis=0
        )
        hidden, d_gate, d_up, part = terms(x, c, *both_w)
        pieces = {
            (at, side): part[i * 2 * rows : (i + 1) * 2 * rows, lo:hi]
            for i, at in enumerate(group)
            for side, lo, hi in sides
        }
        parts.update(lax.optimization_barrier(pieces))
        hs.append(hidden)
        gs.append(d_gate)
        us.append(d_up)
        xs.append(x)
        cs.append(c)

    totals = []
    for side, _, _ in sides:
        p = {at: parts[at, side] for at in range(-3, 5)}
        up = shift(p[4][:rows], 1)
        up = jnp.concatenate([added(p[3][:rows], up), p[3][rows:]], axis=0)
        down = shift(p[4][rows:], -1)
        down = jnp.concatenate([p[-3][:rows], added(p[-3][rows:], down)], axis=0)
        for step in (2, 1):
            up = added(p[step], shift(up, 1))
            down = added(p[-step], shift(down, -1))
        totals.append(
            p[0].astype(jnp.float32)
            + shift(up, 1).astype(jnp.float32)
            + shift(down, -1).astype(jnp.float32)
        )
    total = jnp.concatenate(totals, axis=1)
    other = across(total[rows:].astype(jnp.bfloat16))
    slot_grad = (total[:rows] + other.astype(jnp.float32)).astype(jnp.bfloat16)
    returned = lax.all_to_all(
        slot_grad.reshape(window, CAP, width), "expert", split_axis=0, concat_axis=0, tiled=True
    )
    returned = returned.reshape(window * CAP, width)
    token_grad = matmul(select, returned, ((0,), (0,))).astype(jnp.bfloat16)

    x_all, c_all = (jnp.concatenate(v, axis=0) for v in (xs, cs))
    grads = []
    for left, right in ((gs, x_all), (us, x_all), (hs, c_all)):
        left = jnp.concatenate(left, axis=0)
        theirs = matmul(left[:, units:], right, ((0,), (0,)))
        came = partner(theirs.astype(jnp.bfloat16))
        mine = matmul(left[:, :units], right, ((0,), (0,)))
        grads.append((mine + came.astype(jnp.float32)).astype(jnp.bfloat16)[None])
    return (token_grad, *grads)


def solution(mesh):
    split = Mesh(mesh.devices.reshape(2, 8, 2, mesh.shape["expert"]), DP_EXPERT)
    tok = P(DP_EXPERT, None)
    wts = P("expert", DP, None)
    return jax.shard_map(
        shards,
        mesh=split,
        in_specs=(tok, tok, tok, tok, wts, wts, wts),
        out_specs=(tok, wts, wts, wts),
        check_vma=False,
    )
```
